32 devices in a mesh: img: 8 (over y, x, core), head: 4 (over z).
Axes of the slice: x: 2, y: 2, z: 4, core: 2. Of those that a mesh axis runs over, the one named last changes fastest.
Arguments:
- tokens: bfloat16 [40, 256, 768], P('img'), may hold values from -6 to 6
- mask_embed: float32 [768], replicated, may hold values from -6 to 6
- norm_gains: float32 [2, 768], replicated, may hold values from 0.1 to 1.9
- norm_shifts: float32 [2, 768], replicated, may hold values from -4 to 4
- qkv_weight: bfloat16 [3, 768, 768], P(None, None, 'head'), may hold values from -0.3125 to 0.3125
- qv_bias: float32 [2, 768], P(None, 'head'), may hold values from -4 to 4
- out_weight: bfloat16 [768, 768], P('head'), may hold values from -0.4375 to 0.4375
- output_biases: float32 [2, 768], replicated, may hold values from -4 to 4
- up_weight: bfloat16 [768, 3072], P(None, 'head'), may hold values from -0.21875 to 0.21875
- up_bias: float32 [3072], P('head'), may hold values from -4 to 4
- down_weight: bfloat16 [3072, 768], P('head'), may hold values from -0.109375 to 0.109375
- counts: int32 [40], P('img'), may hold values from 1 to 256, as said below
- token_ranks: int32 [40, 256], P('img'), may hold values from 0 to 255, each once within a row
- cotangent: bfloat16 [40, 256, 768], P('img'), may hold values from -6 to 6
Outputs:
- out: bfloat16 [40, 256, 768], P('img')
- tokens_grad: float32 [40, 256, 768], P('img')
- mask_embed_grad: float32 [768], replicated
- norm_gains_grad: float32 [2, 768], replicated
- norm_shifts_grad: float32 [2, 768], replicated
- qkv_weight_grad: float32 [3, 768, 768], P(None, None, 'head')
- qv_bias_grad: float32 [2, 768], P(None, 'head')
- out_weight_grad: float32 [768, 768], P('head')
- output_biases_grad: float32 [2, 768], replicated
- up_weight_grad: float32 [768, 3072], P(None, 'head')
- up_bias_grad: float32 [3072], P('head')
- down_weight_grad: float32 [3072, 768], P('head')
The draws below stay inside these ranges and needn't reach their ends.
Inputs may be any that keep to these rules, and one draw needn't show every extreme that they name: `counts`: each image's count follows the cosine masking plan over 256 tokens. `token_ranks`: each image's row is a permutation of 0 to 255.
All inputs are finite; a program needn't handle non-finite values.
Results may differ from the reference program's by a relative error of at most 0.012.
The reference program's roundings to bfloat16 on the way count: a program that leaves them out, or rounds other values in their place, can miss the bound.
Values sent between devices are 32-bit elements; how exact they have to be, the bound alone decides.
No kernel may reach another device: no remote copies, remote signals or barrier semaphores. Data moves between devices by JAX's collectives and lax.ppermute only.
A program may use at most 128 MiB of HBM per device.

```python
import jax
import jax.numpy as jnp
import numpy as np
from jax import lax

D = 768
HEADS = 16
HEAD_DIM = 48
FF = 3072
SEQ = 256
IMAGES = 40


def draw_counts(key, part):
    positions = np.arange(SEQ)
    plan = np.maximum(1.0, np.ceil(SEQ * np.cos(np.pi / 2.0 * (positions + 0.5) / SEQ))).astype(np.int32)
    table = jnp.asarray(plan)
    window = max(SEQ // 4, 1)
    image_index = jnp.arange(IMAGES, dtype=jnp.int32)
    lowest = image_index * (SEQ - window) // IMAGES
    offsets = jax.random.randint(jax.random.fold_in(key, 17), (IMAGES,), 0, window, dtype=jnp.int32)
    return table[lowest + offsets]


def steps_of(key, extent, cuts, least, top_value):
    gain, own = 1.0, jax.random.fold_in(key, 6)
    for position, blocks in cuts:
        heights = jnp.exp(jax.random.uniform(jax.random.fold_in(own, position), (blocks,), jnp.float32, least / len(cuts), top_value / len(cuts)))
        gain = gain * jnp.repeat(heights, extent[position] // blocks).reshape([-1 if axis == position else 1 for axis in range(len(extent))])
    return gain


def centred(rng, extent, scale, most, split=(), kind=jnp.bfloat16):
    gain = steps_of(rng, extent, split, -0.22, 0.18) if split else 1.0
    drawn = jax.random.normal(rng, extent, jnp.float32) * scale * gain
    return jnp.minimum(jnp.maximum(drawn, -most), most).astype(kind)


def setup_inputs(seed: int = 0) -> dict:
    streams_of = jax.random.split(jax.random.key(seed), 15)
    tokens = centred(streams_of[0], (IMAGES, SEQ, D), 1.0, 6.0, ((0, 8),))
    mask_embed = centred(streams_of[1], (D,), 1.0, 6.0, (), jnp.float32)
    norm_gains = jnp.clip(1.0 + 0.18 * jax.random.normal(streams_of[2], (2, D), jnp.float32), 0.1, 1.9)
    norm_shifts = centred(streams_of[3], (2, D), 0.3, 4.0, (), jnp.float32)
    qkv_weight = centred(streams_of[4], (3, D, D), (D // 2) ** -0.5, 0.3125, ((2, 4),))
    qv_bias = centred(streams_of[5], (2, D), 0.3, 4.0, ((1, 4),), jnp.float32)
    out_weight = centred(streams_of[6], (D, D), (D // 4) ** -0.5, 0.4375, ((0, 4),))
    output_biases = centred(streams_of[7], (2, D), 0.3, 4.0, (), jnp.float32)
    up_weight = centred(streams_of[8], (D, FF), D ** -0.5, 0.21875, ((1, 4),))
    up_bias = centred(streams_of[9], (FF,), 0.3, 4.0, ((0, 4),), jnp.float32)
    down_weight = centred(streams_of[10], (FF, D), FF ** -0.5, 0.109375, ((0, 4),))
    counts = draw_counts(jax.random.fold_in(streams_of[14], 71), 0)
    token_ranks = jax.vmap(lambda own: jax.random.permutation(own, SEQ))(jax.random.split(streams_of[12], IMAGES)).reshape((IMAGES, SEQ)).astype(jnp.int32)
    cotangent = centred(streams_of[13], (IMAGES, SEQ, D), 1.0, 6.0, ((0, 8),))
    return dict(tokens=tokens, mask_embed=mask_embed, norm_gains=norm_gains, norm_shifts=norm_shifts, qkv_weight=qkv_weight, qv_bias=qv_bias, out_weight=out_weight, output_biases=output_biases, up_weight=up_weight, up_bias=up_bias, down_weight=down_weight, counts=counts, token_ranks=token_ranks, cotangent=cotangent)


norm_eps = 1e-06
highest = lax.Precision.HIGHEST

@jax.custom_vjp
def low(v):
    return lax.optimization_barrier(v.astype(jnp.bfloat16)).astype(jnp.float32)

@jax.custom_vjp
def low_back(v):
    return v

def low_keep(v):
    return (low(v), None)

def low_pass(kept, grad):
    return (grad,)

def back_keep(v):
    return (v, None)

def back_low(kept, grad):
    return (low(grad),)
low.defvjp(low_keep, low_pass)
low_back.defvjp(back_keep, back_low)

def normalize(values, scaling, offset):
    center = values - lax.optimization_barrier(jnp.mean(values, axis=-1, keepdims=True))
    inverse = lax.rsqrt(lax.optimization_barrier(jnp.mean(center * center, axis=-1, keepdims=True)) + norm_eps)
    return center * inverse * scaling + offset

def block(params, inputs, masked_now):
    mask_embed, norm_gains, norm_shifts, qkv_weight, qv_bias, out_weight, output_biases, up_weight, up_bias, down_weight = params
    group_size, seq_len, model_width = inputs.shape
    row_count = group_size * seq_len
    score_scale = HEAD_DIM ** (-0.5)
    start = jnp.where(masked_now[:, :, None] > 0, mask_embed[None, None, :], inputs).reshape(row_count, model_width)
    attn_normed = low(normalize(start, norm_gains[0], norm_shifts[0]))
    bias_rows = jnp.stack([qv_bias[0], jnp.zeros_like(qv_bias[0]), qv_bias[1]])
    projected = jnp.einsum('td,ndc->ntc', attn_normed, qkv_weight, precision=highest) + bias_rows[:, None, :]
    projected = low(low_back(projected))
    head_shape = (group_size, seq_len, HEADS, HEAD_DIM)
    queries = projected[0].reshape(head_shape)
    keys_all = projected[1].reshape(head_shape)
    values_all = projected[2].reshape(head_shape)
    raw_scores = low_back(jnp.einsum('bqhd,bkhd->bhqk', queries, keys_all, precision=highest))
    attn_probs = low(jax.nn.softmax(raw_scores * score_scale, axis=-1))
    mixed = jnp.einsum('bhqk,bkhd->bqhd', attn_probs, values_all, precision=highest).reshape(row_count, model_width)
    mixed = low(low_back(mixed))
    after_attn = start + low_back(jnp.dot(mixed, out_weight, precision=highest)) + output_biases[0]
    mlp_normed = low(normalize(after_attn, norm_gains[1], norm_shifts[1]))
    pre_act = low_back(jnp.dot(mlp_normed, up_weight, precision=highest) + up_bias)
    activated = low(jax.nn.gelu(pre_act, approximate=True))
    after_mlp = after_attn + low_back(jnp.dot(activated, down_weight, precision=highest)) + output_biases[1]
    return after_mlp.reshape(group_size, seq_len, model_width)

def reference(tokens, mask_embed, norm_gains, norm_shifts, qkv_weight, qv_bias, out_weight, output_biases, up_weight, up_bias, down_weight, counts, token_ranks, cotangent):
    masked = (token_ranks < counts[:, None]).astype(jnp.float32)
    masked_sum = jnp.sum(counts.astype(jnp.float32))
    loss_scale = IMAGES * SEQ / masked_sum
    params = (mask_embed, norm_gains, norm_shifts, qkv_weight.astype(jnp.float32), qv_bias, out_weight.astype(jnp.float32), output_biases, up_weight.astype(jnp.float32), up_bias, down_weight.astype(jnp.float32))
    group_size = 8
    steps_count = IMAGES // group_size
    inputs = tokens.astype(jnp.float32).reshape(steps_count, group_size, SEQ, D)
    mask_groups = masked.reshape(steps_count, group_size, SEQ)
    seeds = cotangent.astype(jnp.float32).reshape(steps_count, group_size, SEQ, D)

    def one_group(running, pieces):
        inputs_now, mask_now, seed_now = pieces
        result, pullback = jax.vjp(lambda weights, values: block(weights, values, mask_now), params, inputs_now)
        grad_params, grad_inputs = pullback(seed_now * mask_now[:, :, None])
        running = jax.tree.map(jnp.add, running, grad_params)
        return (running, (result, grad_inputs))
    zero_grads = jax.tree.map(jnp.zeros_like, params)
    summed, (outputs, input_grads) = lax.scan(one_group, zero_grads, (inputs, mask_groups, seeds))
    scaled = jax.tree.map(lambda grad_value: grad_value * loss_scale, summed)
    out = outputs.reshape(IMAGES, SEQ, D).astype(jnp.bfloat16)
    tokens_grad = input_grads.reshape(IMAGES, SEQ, D) * loss_scale
    return (out, tokens_grad, scaled[0], scaled[1], scaled[2], scaled[3], scaled[4], scaled[5], scaled[6], scaled[7], scaled[8], scaled[9])
```

```python
import jax
import jax.numpy as jnp
from jax import lax
from jax.sharding import PartitionSpec as P

HEAD_DIM = 48
norm_eps = 1e-06
f32 = jnp.float32
bf16 = jnp.bfloat16


def contract_rows(left, right):
    return lax.dot_general(left, right, (((0,), (0,)), ((), ())), preferred_element_type=f32)


def times_transposed(left, right):
    return lax.dot_general(left, right, (((1,), (1,)), ((), ())), preferred_element_type=f32)


def times(left, right):
    return jnp.dot(left, right, preferred_element_type=f32)


def normal_of(values):
    center = values - jnp.mean(values, axis=-1, keepdims=True)
    inverse = lax.rsqrt(jnp.mean(center * center, axis=-1, keepdims=True) + norm_eps)
    return center * inverse, inverse


def normalize_back(upstream, normal, inverse, scaling):
    scaled = upstream * scaling
    inner = (
        scaled
        - jnp.mean(scaled, axis=-1, keepdims=True)
        - normal * jnp.mean(scaled * normal, axis=-1, keepdims=True)
    )
    return inverse * inner


def head_sum(part):
    if lax.axis_size("head") != 4:
        return lax.psum(part, "head")
    place = lax.axis_index("head")
    inner = (place == 1) | (place == 2)
    half = part + lax.ppermute(part, "head", [(0, 1), (3, 2)])
    total = half + lax.ppermute(half, "head", [(1, 2), (2, 1)])
    return jnp.where(inner, total, lax.ppermute(total, "head", [(1, 0), (2, 3)]))


def gelu_and_slope(v):
    k = 0.7978845608028654
    th = jnp.tanh(k * (v + 0.044715 * (v * v * v)))
    act = 0.5 * v * (1.0 + th)
    slope = 0.5 * (1.0 + th) + 0.5 * v * (1.0 - th * th) * (k * (1.0 + 3 * 0.044715 * (v * v)))
    return act, slope


def per_device(
    tokens, mask_embed, norm_gains, norm_shifts, qkv_weight, qv_bias, out_weight, output_biases,
    up_weight, up_bias, down_weight, counts, token_ranks, cotangent,
):
    images, seq_len, model_width = tokens.shape
    local_width = qkv_weight.shape[2]
    heads = local_width // HEAD_DIM
    scale = HEAD_DIM ** (-0.5)
    split = lambda m: m.reshape(seq_len, heads, HEAD_DIM).transpose(1, 0, 2)
    merge = lambda m: m.transpose(1, 0, 2).reshape(seq_len, local_width)
    bdot = lambda a, b, ca, cb: lax.dot_general(
        a, b, (((ca,), (cb,)), ((0,), (0,))), preferred_element_type=f32
    )

    masked_sum = lax.psum(jnp.sum(counts.astype(f32)), "img")
    loss_scale = lax.axis_size("img") * images * seq_len / masked_sum
    is_masked = token_ranks < counts[:, None]

    st = []
    for b in range(images):
        mask = is_masked[b][:, None]
        start = jnp.where(mask, mask_embed[None, :], tokens[b].astype(f32))
        normal, inverse = normal_of(start)
        normed = (normal * norm_gains[0] + norm_shifts[0]).astype(bf16)
        q = split((times(normed, qkv_weight[0]) + qv_bias[0]).astype(bf16))
        k = split(times(normed, qkv_weight[1]).astype(bf16))
        v = split((times(normed, qkv_weight[2]) + qv_bias[1]).astype(bf16))
        scores = bdot(q, k, 2, 2) * scale
        ex = jnp.exp(scores - jnp.max(scores, axis=-1, keepdims=True))
        probs = ex / jnp.sum(ex, axis=-1, keepdims=True)
        mixed = merge(bdot(probs.astype(bf16), v, 2, 1)).astype(bf16)
        attended = head_sum(times(mixed, out_weight))
        st.append(dict(mask=mask.astype(f32), start=start, normal=normal, inverse=inverse,
                       normed=normed, q=q, k=k, v=v, probs=probs, mixed=mixed, attended=attended))
    for b, s in enumerate(st):
        after = s["start"] + s["attended"] + output_biases[0]
        normal, inverse = normal_of(after)
        normed = (normal * norm_gains[1] + norm_shifts[1]).astype(bf16)
        act, slope = gelu_and_slope(times(normed, up_weight) + up_bias)
        act = act.astype(bf16)
        signal = cotangent[b].astype(f32) * s["mask"]
        signal_low = signal.astype(bf16)
        grad_pre = (times_transposed(signal_low, down_weight) * slope).astype(bf16)
        grad_normed = head_sum(times_transposed(grad_pre, up_weight))
        s.update(after=after, normal2=normal, inverse2=inverse, normed2=normed, act=act,
                 signal=signal, signal_low=signal_low, grad_pre=grad_pre, grad_normed2=grad_normed)
    for b, s in enumerate(st):
        upper = s["signal"] + normalize_back(s["grad_normed2"], s["normal2"], s["inverse2"], norm_gains[1])
        upper_low = upper.astype(bf16)
        gm = split(times_transposed(upper_low, out_weight).astype(bf16))
        probs = s["probs"]
        gp = bdot(gm, s["v"], 2, 2)
        gv = merge(bdot(probs.astype(bf16), gm, 1, 1)).astype(bf16)
        gs = (probs * (gp - jnp.sum(probs * gp, axis=-1, keepdims=True)) * scale).astype(bf16)
        gq = merge(bdot(gs, s["k"], 2, 1)).astype(bf16)
        gk = merge(bdot(gs, s["q"], 1, 1)).astype(bf16)
        back = (times_transposed(gq, qkv_weight[0]) + times_transposed(gk, qkv_weight[1])
                + times_transposed(gv, qkv_weight[2]))
        s.update(upper=upper, upper_low=upper_low, gq=gq, gk=gk, gv=gv, grad_normed1=head_sum(back))
    for b, s in enumerate(st):
        s["branch"] = head_sum(times(s["act"], down_weight))
        s["out"] = (s["after"] + s["branch"] + output_biases[1]).astype(bf16)

    cat = lambda name: jnp.concatenate([s[name] for s in st], axis=0)
    down_raw = contract_rows(cat("act"), cat("signal_low"))
    up_raw = contract_rows(cat("normed2"), cat("grad_pre"))
    down_raw, up_raw = lax.psum((down_raw, up_raw), "img")
    out_raw = contract_rows(cat("mixed"), cat("upper_low"))
    normed1 = cat("normed")
    qkv_raw = jnp.stack([contract_rows(normed1, cat(n)) for n in ("gq", "gk", "gv")])
    out_raw, qkv_raw = lax.psum((out_raw, qkv_raw), "img")

    total = lambda f: sum(f(s) for s in st)
    sums = lambda m: jnp.sum(m.astype(f32), axis=0)
    for s in st:
        grad = normalize_back(s["grad_normed1"], s["normal"], s["inverse"], norm_gains[0])
        s["lower"] = s["upper"] + grad
    small = [
        total(lambda s: sums(s["lower"] * s["mask"])),
        total(lambda s: sums(s["grad_normed1"] * s["normal"])),
        total(lambda s: sums(s["grad_normed2"] * s["normal2"])),
        total(lambda s: sums(s["grad_normed1"])),
        total(lambda s: sums(s["grad_normed2"])),
        total(lambda s: sums(s["upper"])),
        total(lambda s: sums(s["signal"])),
    ]
    small = jnp.stack(small)
    bias = jnp.concatenate([total(lambda s: sums(s["gq"])), total(lambda s: sums(s["gv"])),
                            total(lambda s: sums(s["grad_pre"]))])
    small, bias = lax.psum((small, bias), "img")
    small = small * loss_scale
    bias = bias * loss_scale
    out = jnp.stack([s["out"] for s in st])
    tokens_grad = jnp.stack([s["lower"] * ((1.0 - s["mask"]) * loss_scale) for s in st])
    return (
        out,
        tokens_grad,
        small[0],
        small[1:3],
        small[3:5],
        qkv_raw * loss_scale,
        bias[: 2 * local_width].reshape(2, local_width),
        out_raw * loss_scale,
        small[5:7],
        up_raw * loss_scale,
        bias[2 * local_width :],
        down_raw * loss_scale,
    )


def solution(mesh):
    return jax.shard_map(
        per_device,
        mesh=mesh,
        in_specs=(
            P("img", None, None), P(), P(), P(), P(None, None, "head"), P(None, "head"),
            P("head", None), P(), P(None, "head"), P("head"), P("head", None), P("img"),
            P("img", None), P("img", None, None),
        ),
        out_specs=(
            P("img", None, None), P("img", None, None), P(), P(), P(), P(None, None, "head"),
            P(None, "head"), P("head", None), P(), P(None, "head"), P("head"), P("head", None),
        ),
        check_vma=False,
    )
```
